32 devices in a mesh: gx: 2 (over x), gy: 4 (over y, core), gz: 4 (over z).
Axes of the slice: x: 2, y: 2, z: 4, core: 2. Of those that a mesh axis runs over, the one named last changes fastest.
Arguments:
- vectors: bfloat16 [2, 3, 8, 16, 16, 256], P(None, None, 'gx', 'gy', 'gz'), may hold values from -6 to 6
- gauge_links: float32 [3, 2, 3, 3, 8, 16, 16], P(None, None, None, None, 'gx', 'gy', 'gz'), may hold values from -2.5 to 2.5
- momenta: int32 [2, 3], replicated, may hold values from 1 to 3
- perambulator: bfloat16 [32, 2, 256, 4, 256], P(('gx', 'gy', 'gz')), may hold values from -0.19921875 to 0.19921875
Outputs:
- smeared: bfloat16 [2, 3, 8, 16, 16, 256], P(None, None, 'gx', 'gy', 'gz')
- sandwich: bfloat16 [32, 2, 2, 256, 256], P(('gx', 'gy', 'gz'))
The draws below stay inside these ranges and needn't reach their ends.
All inputs are finite; a program needn't handle non-finite values.
Results may differ from the reference program's by a relative error of at most 0.0074.
Values may be sent and summed in bfloat16 or wider, within the bound.
A program may use at most 64 MiB of HBM per device.

```python
import math
import jax
import jax.numpy as jnp
from jax import lax

NVEC = 256
NMOM = 2
NSPIN = 4
PCOL = 256
NX = 8
NY = 16
NZ = 16
PERAM = 32


def set_ends(values, own_key, smallest, top_value):
    dims = values.shape
    place = [jax.random.randint(jax.random.fold_in(own_key, axis), (), 0, dims[axis]) for axis in range(len(dims))]
    values = values.at[tuple(place)].set(smallest)
    longest = dims.index(max(dims))
    place[longest] = (place[longest] + 1) % dims[longest]
    return values.at[tuple(place)].set(top_value)


def shard_levels(key, extent, pieces, smallest, top_value):
    level, own = 1.0, jax.random.fold_in(key, 6)
    for axis_at, shards_of in pieces:
        steps = jnp.exp(jax.random.uniform(jax.random.fold_in(own, axis_at), (shards_of,), jnp.float32, smallest / len(pieces), top_value / len(pieces)))
        level = level * jnp.repeat(steps, extent[axis_at] // shards_of).reshape([-1 if axis == axis_at else 1 for axis in range(len(extent))])
    return level


def centred(rng, dims, spread, limit, pieces=(), held_as=jnp.bfloat16):
    level = shard_levels(rng, dims, pieces, -0.22, 0.18) if pieces else 1.0
    array = jax.random.normal(rng, dims, jnp.float32) * spread * level
    return jnp.minimum(jnp.maximum(array, -limit), limit).astype(held_as)


def setup_inputs(seed: int = 0) -> dict:
    arg_keys = jax.random.split(jax.random.key(seed), 5)
    return {
        "vectors": centred(arg_keys[0], (2, 3, NX, NY, NZ, NVEC), 1.0, 6.0, ((2, 2), (3, 4), (4, 4))),
        "gauge_links": centred(arg_keys[1], (3, 2, 3, 3, NX, NY, NZ), 6 ** -0.5, 2.5, ((4, 2), (5, 4), (6, 4)), jnp.float32),
        "momenta": set_ends(jax.random.randint(arg_keys[2], (NMOM, 3), 1, 4), jax.random.fold_in(arg_keys[2], 1), 1, 3).astype(jnp.int32),
        "perambulator": centred(arg_keys[3], (PERAM, 2, NVEC, NSPIN, PCOL), 0.03125, 0.19921875, ((0, 32),)),
    }


def link_times(link_mu, colour_field, adjoint):
    real_part = None
    imag_part = None
    for column in range(3):
        if adjoint:
            link_real = link_mu[0][column]
            link_imag = -link_mu[1][column]
        else:
            link_real = link_mu[0][:, column]
            link_imag = link_mu[1][:, column]
        link_real = link_real[..., None]
        link_imag = link_imag[..., None]
        field_real = colour_field[0][column]
        field_imag = colour_field[1][column]
        add_real = link_real * field_real - link_imag * field_imag
        add_imag = link_real * field_imag + link_imag * field_real
        real_part = add_real if real_part is None else real_part + add_real
        imag_part = add_imag if imag_part is None else imag_part + add_imag
    return jnp.stack([real_part, imag_part])

def neighbour_full(colour_field, gauge_links):
    summed = None
    for axis_mu in range(3):
        above = jnp.roll(colour_field, -1, axis=2 + axis_mu)
        below = jnp.roll(colour_field, 1, axis=2 + axis_mu)
        link_here = gauge_links[axis_mu]
        link_below = jnp.roll(link_here, 1, axis=3 + axis_mu)
        hop_term = link_times(link_here, above, False) + link_times(link_below, below, True)
        summed = hop_term if summed is None else summed + hop_term
    return summed

def rounded(value):
    return lax.optimization_barrier(value.astype(jnp.bfloat16)).astype(jnp.float32)

def phase_tables(momenta, pos_x, pos_y, pos_z, cells_x, cells_y, cells_z):
    frac_x = (momenta[:, 0:1] * pos_x[None, :] % cells_x).astype(jnp.float32) / cells_x
    frac_y = (momenta[:, 1:2] * pos_y[None, :] % cells_y).astype(jnp.float32) / cells_y
    frac_z = (momenta[:, 2:3] * pos_z[None, :] % cells_z).astype(jnp.float32) / cells_z
    lattice_fraction = frac_x[:, :, None, None] + frac_y[:, None, :, None] + frac_z[:, None, None, :]
    theta = 2.0 * math.pi * lattice_fraction
    return (jnp.cos(theta), jnp.sin(theta))

def reference(vectors, gauge_links, momenta, perambulator):
    block_count = NVEC // 32
    blocks = jnp.moveaxis(vectors.reshape(2, 3, NX, NY, NZ, block_count, 32), 5, 0)

    def smear_block(vector_block):
        initial_recursion = rounded(neighbour_full(vector_block, gauge_links) / 6.0)
        second = neighbour_full(initial_recursion, gauge_links)
        return (2.0 * second / 6.0 - vector_block.astype(jnp.float32)).astype(jnp.bfloat16)
    smeared_blocks = lax.map(smear_block, blocks)
    smeared = jnp.moveaxis(smeared_blocks, 0, 5).reshape(2, 3, NX, NY, NZ, NVEC)
    pos_y = jnp.arange(NY, dtype=jnp.int32)
    pos_z = jnp.arange(NZ, dtype=jnp.int32)

    def slab_step(running, x_index):
        x_slab = lax.dynamic_index_in_dim(smeared, x_index, axis=2, keepdims=False).astype(jnp.float32)
        cos_table, sin_table = phase_tables(momenta, x_index[None], pos_y, pos_z, NX, NY, NZ)
        cos_b = cos_table[:, 0][:, None, :, :, None]
        sin_b = sin_table[:, 0][:, None, :, :, None]
        real_w = x_slab[0][None]
        imag_w = x_slab[1][None]
        real_z = rounded(cos_b * real_w + sin_b * imag_w)
        imag_z = rounded(cos_b * imag_w - sin_b * real_w)
        right_side = jnp.stack([jnp.stack([real_z, imag_z], 1), jnp.stack([imag_z, -real_z], 1)], 0)
        slab_term = jnp.einsum('cmpjyzb,pjyza->cmba', right_side, x_slab, precision=lax.Precision.HIGHEST)
        return (running + slab_term, None)
    start = jnp.zeros((2, NMOM, NVEC, NVEC), jnp.float32)
    summed, unused = lax.scan(slab_step, start, jnp.arange(NX, dtype=jnp.int32))
    norm_scale = 1.0 / math.sqrt(3.0 * NX * NY * NZ)
    elementals_low = rounded(summed * norm_scale)

    def sandwich_one(single):
        peram_real = single[0].astype(jnp.float32)
        peram_imag = single[1].astype(jnp.float32)
        left_side = jnp.stack([jnp.stack([peram_real, -peram_imag]), jnp.stack([peram_imag, peram_real])])
        inner = rounded(jnp.einsum('cmba,cdask->mbdsk', elementals_low, left_side, precision=lax.Precision.HIGHEST))
        right_peram = jnp.stack([jnp.stack([peram_real, peram_imag]), jnp.stack([-peram_imag, peram_real])])
        outcome = jnp.einsum('mbcsk,cdbsl->mdkl', inner, right_peram, precision=lax.Precision.HIGHEST)
        return outcome.astype(jnp.bfloat16)
    sandwich = lax.map(sandwich_one, perambulator)
    return (smeared, sandwich)
```

```python
import functools
import math

import jax
import jax.numpy as jnp
import numpy as np
from jax import lax
from jax.experimental import pallas as pl
from jax.experimental.pallas import tpu as pltpu
from jax.sharding import PartitionSpec as P

AXES = ("gx", "gy", "gz")
MESH = pl.DeviceIdType.MESH
F32 = jnp.float32
BF16 = jnp.bfloat16


class Plan:
    def __init__(self, dims):
        self.dims = dims
        self.sites = int(np.prod(dims))
        grid = np.indices(dims).reshape(3, -1)
        strides = (dims[1] * dims[2], dims[2], 1)
        self.face = [self.sites // dims[mu] for mu in range(3)]
        offset, self.slot = 0, []
        for mu in range(3):
            for _ in range(2):
                self.slot.append(offset)
                offset += self.face[mu]
        self.halo = offset
        self.cols = -(-(self.sites + offset) // 128) * 128
        offset, self.ghost = 0, []
        for mu in range(3):
            self.ghost.append(offset)
            offset += self.face[mu]
        self.ghosts = offset
        self.link_rows = -(-(self.sites + offset) // 16) * 16
        code = np.zeros((self.sites, self.cols), np.int32)
        pick = np.zeros((self.halo, self.sites), np.float32)
        pick_link = np.zeros((self.ghosts, self.sites), np.float32)
        below = np.zeros((3 * self.sites, self.link_rows), np.float32)
        for mu in range(3):
            others = [a for a in range(3) if a != mu]
            for s in range(self.sites):
                at = grid[:, s]
                f = at[others[0]] * dims[others[1]] + at[others[1]]
                if at[mu] == dims[mu] - 1:
                    code[s, self.sites + self.slot[2 * mu] + f] = 2 * mu + 1
                    pick[self.slot[2 * mu + 1] + f, s] = 1
                    pick_link[self.ghost[mu] + f, s] = 1
                else:
                    code[s, s + strides[mu]] = 2 * mu + 1
                if at[mu] == 0:
                    code[s, self.sites + self.slot[2 * mu + 1] + f] = 2 * mu + 2
                    pick[self.slot[2 * mu] + f, s] = 1
                    below[mu * self.sites + s, self.sites + self.ghost[mu] + f] = 1
                else:
                    code[s, s - strides[mu]] = 2 * mu + 2
                    below[mu * self.sites + s, s - strides[mu]] = 1
        self.code, self.pick, self.pick_link, self.below = code, pick, pick_link, below


def dot(a, b):
    return jnp.dot(a, b, preferred_element_type=F32)


def main_kernel(plan, counts, scale, reduce_here, *refs):
    (v_ref, lt_ref, tab_ref, code_ref, pick_ref, pickl_ref, below_ref, smeared_ref, out_ref,
     v1, v2, pk1, pk2, lk, lg, mh, ml, acc, half_out, half_in, plane_out, plane_in, z_out, z_in,
     ssem, rsem) = refs
    sites, cols, parts = plan.sites, plan.cols, 6
    me = [lax.axis_index(a) for a in AXES]
    nx, ny, nz = counts

    def neighbour(mu, step):
        at = list(me)
        at[mu] = lax.rem(at[mu] + step + counts[mu], counts[mu])
        return tuple(at)

    ny2 = ny // 2
    nq = nx * ny2
    h = lax.rem(me[1], 2)
    q = me[0] * ny2 + me[1] // 2
    partner = (me[0], me[1] + 1 - 2 * h, me[2])

    def plane_at(index):
        return (index // ny2, lax.rem(index, ny2) * 2 + h, me[2])

    greeted = [neighbour(mu, step) for mu in range(3) for step in (-1, 1)]
    if reduce_here:
        greeted += [partner]
        greeted += [plane_at(lax.rem(q + r, nq)) for r in range(1, nq)]
        greeted += [(me[0], me[1], lax.rem(me[2] + r, nz)) for r in range(1, nz)]
    barrier = pltpu.get_barrier_semaphore()
    for device in greeted:
        pl.semaphore_signal(barrier, inc=1, device_id=device, device_id_type=MESH)

    used = [0]

    def copy(src, dst, device):
        k = used[0]
        used[0] += 1
        return pltpu.make_async_remote_copy(
            src_ref=src, dst_ref=dst, send_sem=ssem.at[k], recv_sem=rsem.at[k],
            device_id=device, device_id_type=MESH)

    pick = pick_ref[...]

    def fill(buf, packed, part, value):
        buf[part, 0:sites, :] = value
        packed[part] = dot(pick, value).astype(BF16)

    rest = sites + plan.halo
    for buf in (v1, v2):
        if rest < cols:
            buf[:, rest:cols, :] = jnp.zeros((parts, cols - rest, buf.shape[2]), BF16)
    lt = lt_ref[...]
    lk[...] = dot(pickl_ref[...], lt).astype(BF16)
    lg[0:sites, :] = lt
    used_rows = sites + plan.ghosts
    if used_rows < plan.link_rows:
        lg[used_rows:, :] = jnp.zeros((plan.link_rows - used_rows, lg.shape[1]), BF16)
    for part in range(parts):
        fill(v1, pk1, part, v_ref[part])
    pl.semaphore_wait(barrier, len(greeted))

    sends = []
    links = []
    for mu in range(3):
        g, n = plan.ghost[mu], plan.face[mu]
        links.append(copy(lk.at[g:g + n, :], lg.at[sites + g:sites + g + n, :], neighbour(mu, 1)))
        links[-1].start()

    def exchange(packed, buf):
        made = []
        for mu in (2, 0, 1):
            for side in range(2):
                o, n = plan.slot[2 * mu + side], plan.face[mu]
                made.append(copy(packed.at[:, o:o + n, :],
                                 buf.at[:, sites + o:sites + o + n, :],
                                 neighbour(mu, 2 * side - 1)))
                made[-1].start()
        return made

    halo1 = exchange(pk1, v1)
    for c in links:
        c.wait_recv()
    sends += links
    down = dot(below_ref[...], lg[...])
    here = lt.astype(F32)
    masks = [code_ref[...] == d + 1 for d in range(6)]
    shape = (sites, cols)
    for part, store in ((0, mh), (1, ml)):
        for i in range(3):
            for j in range(3):
                for c in range(2):
                    total = jnp.zeros(shape, F32)
                    for mu in range(3):
                        k = part * 128 + ((mu * 2 + c) * 3 + i) * 3 + j
                        value = here[:, k:k + 1]
                        total = jnp.where(masks[2 * mu], jnp.broadcast_to(value, shape), total)
                        k = part * 128 + ((mu * 2 + c) * 3 + j) * 3 + i
                        value = down[mu * sites:(mu + 1) * sites, k:k + 1]
                        if c:
                            value = -value
                        total = jnp.where(masks[2 * mu + 1], jnp.broadcast_to(value, shape), total)
                    total = total.astype(BF16)

                    def put(ro, co, val):
                        r0, c0 = (ro * 3 + i) * sites, (co * 3 + j) * cols
                        store[r0:r0 + sites, c0:c0 + cols] = val

                    if c == 0:
                        put(0, 0, total)
                        put(1, 1, total)
                    else:
                        put(1, 0, total)
                        put(0, 1, -total)

    def hop(buf):
        field = buf[...].reshape(parts * cols, buf.shape[2])
        return dot(mh[...], field) + dot(ml[...], field)

    for c in halo1:
        c.wait_recv()
    sends += halo1
    first = (hop(v1) / 6.0).astype(BF16)
    for part in range(parts):
        fill(v2, pk2, part, first[part * sites:(part + 1) * sites])
    halo2 = exchange(pk2, v2)
    for c in halo2:
        c.wait_recv()
    sends += halo2
    vectors = v_ref[...].reshape(parts * sites, v_ref.shape[2]).astype(F32)
    smeared = (2.0 * hop(v2) / 6.0 - vectors).astype(BF16)
    smeared_ref[...] = smeared.reshape(smeared_ref.shape)
    wide = smeared.astype(F32)
    rows = 3 * sites
    real_w, imag_w = wide[:rows], wide[rows:]
    left = jnp.transpose(wide).astype(BF16)
    moms = out_ref.shape[0] // 2
    width = v_ref.shape[2]
    for m in range(moms):
        cos_b = jnp.concatenate([tab_ref[:, 2 * m:2 * m + 1]] * 3, axis=0)
        sin_b = jnp.concatenate([tab_ref[:, 2 * m + 1:2 * m + 2]] * 3, axis=0)
        real_z = (cos_b * real_w + sin_b * imag_w).astype(BF16)
        imag_z = (cos_b * imag_w - sin_b * real_w).astype(BF16)
        acc[m] = dot(left, jnp.concatenate([real_z, imag_z], axis=0)) * scale
        acc[moms + m] = dot(left, jnp.concatenate([imag_z, -real_z], axis=0)) * scale

    if not reduce_here:
        out_ref[...] = acc[...]
        for c in sends:
            c.wait_send()
        return

    chunks = 2 * moms
    half = width // 2
    keep = pl.multiple_of(h * half, half)
    give = pl.multiple_of((1 - h) * half, half)
    half_out[...] = acc[:, pl.ds(give, half), :].astype(BF16)
    c = copy(half_out, half_in, partner)
    c.start()
    c.wait_recv()
    sends.append(c)
    piece = half // nq
    total = acc[:, pl.ds(keep, half), :] + half_in[...].astype(F32)
    acc[:, pl.ds(keep, half), :] = total
    plane_out[...] = total.astype(BF16)
    stage = []
    for r in range(1, nq):
        p = lax.rem(q + r, nq)
        c = copy(plane_out.at[:, pl.ds(pl.multiple_of(p * piece, piece), piece), :],
                 plane_in.at[r - 1], plane_at(p))
        c.start()
        stage.append(c)
    mine = pl.multiple_of(h * half + q * piece, piece)
    total = acc[:, pl.ds(mine, piece), :]
    for r in range(1, nq):
        stage[r - 1].wait_recv()
        total = total + plane_in[r - 1].astype(F32)
    sends += stage
    acc[:, pl.ds(mine, piece), :] = total
    z_out[...] = total.astype(BF16)
    per = chunks // nz
    stage = []
    for r in range(1, nz):
        p = lax.rem(me[2] + r, nz)
        c = copy(z_out.at[pl.ds(p * per, per)], z_in.at[r - 1], (me[0], me[1], p))
        c.start()
        stage.append(c)
    total = acc[pl.ds(me[2] * per, per), pl.ds(mine, piece), :]
    for r in range(1, nz):
        stage[r - 1].wait_recv()
        total = total + z_in[r - 1].astype(F32)
    sends += stage
    out_ref[pl.ds(me[2] * per, per), pl.ds(mine, piece), :] = total.astype(BF16)

    def gather(pairs):
        made = []
        for block, device, _ in pairs:
            made.append(copy(block, block, device))
            made[-1].start()
        for (_, device, back), c, k in zip(pairs, made, range(used[0] - len(made), used[0])):
            pltpu.make_async_remote_copy(
                src_ref=back, dst_ref=back, send_sem=ssem.at[k], recv_sem=rsem.at[k],
                device_id=device, device_id_type=MESH).wait_recv()
        sends.extend(made)

    def z_block(z):
        return out_ref.at[pl.ds(z * per, per), pl.ds(mine, piece), :]

    gather([(z_block(me[2]), (me[0], me[1], lax.rem(me[2] + r, nz)),
             z_block(lax.rem(me[2] + nz - r, nz))) for r in range(1, nz)])

    def plane_block(p):
        return out_ref.at[:, pl.ds(pl.multiple_of(h * half + p * piece, piece), piece), :]

    gather([(plane_block(q), plane_at(lax.rem(q + r, nq)), plane_block(lax.rem(q + nq - r, nq)))
            for r in range(1, nq)])
    gather([(out_ref.at[:, pl.ds(keep, half), :], partner, out_ref.at[:, pl.ds(give, half), :])])
    for c in sends:
        c.wait_send()


def smear_and_project(plan, counts, scale, fields, links, tables, moms):
    parts, sites, width = fields.shape
    chunks = 2 * moms
    nx, ny, nz = counts
    nq = max(nx * (ny // 2), 1)
    half = width // 2
    reduce_here = ny % 2 == 0 and half % (16 * nq) == 0 and chunks % nz == 0 and nz > 1 and nq > 1
    vm = pltpu.VMEM
    if reduce_here:
        extra = [
            vm((chunks, half, width), BF16), vm((chunks, half, width), BF16),
            vm((chunks, half, width), BF16), vm((nq - 1, chunks, half // nq, width), BF16),
            vm((chunks, half // nq, width), BF16),
            vm((nz - 1, chunks // nz, half // nq, width), BF16),
        ]
        copies = 3 + 12 + 2 * (1 + (nq - 1) + (nz - 1))
    else:
        extra = [vm((8, 128), BF16)] * 6
        copies = 3 + 12
    vmem = pl.BlockSpec(memory_space=pltpu.VMEM)
    return pl.pallas_call(
        functools.partial(main_kernel, plan, counts, scale, reduce_here),
        out_shape=(
            jax.ShapeDtypeStruct((parts, sites, width), BF16),
            jax.ShapeDtypeStruct((chunks, width, width), BF16 if reduce_here else F32),
        ),
        in_specs=[vmem] * 7,
        out_specs=(vmem, vmem),
        scratch_shapes=[
            vm((parts, plan.cols, width), BF16), vm((parts, plan.cols, width), BF16),
            vm((parts, plan.halo, width), BF16), vm((parts, plan.halo, width), BF16),
            vm((plan.ghosts, 256), BF16), vm((plan.link_rows, 256), BF16),
            vm((parts * sites, parts * plan.cols), BF16),
            vm((parts * sites, parts * plan.cols), BF16),
            vm((chunks, width, width), F32),
            *extra,
            pltpu.SemaphoreType.DMA((copies,)), pltpu.SemaphoreType.DMA((copies,)),
        ],
        compiler_params=pltpu.CompilerParams(
            collective_id=0, has_side_effects=True, vmem_limit_bytes=48 << 20),
        name="smear_project",
    )(fields, links, tables, jnp.asarray(plan.code), jnp.asarray(plan.pick, BF16),
      jnp.asarray(plan.pick_link, BF16), jnp.asarray(plan.below, BF16)), reduce_here


def sandwich_kernel(moms, spins, cols, ft_ref, p_ref, out_ref, pt, rhs, inner):
    width = p_ref.shape[1]
    for c in range(2):
        for s in range(spins):
            block = p_ref[c, :, s * cols:(s + 1) * cols]
            pt[s * cols:(s + 1) * cols, c * width:(c + 1) * width] = jnp.transpose(block)
    for s in range(spins):
        real_p = p_ref[0, :, s * cols:(s + 1) * cols]
        imag_p = p_ref[1, :, s * cols:(s + 1) * cols]
        r0 = s * 2 * width
        rhs[r0:r0 + width, 0:cols] = real_p
        rhs[r0:r0 + width, cols:2 * cols] = imag_p
        rhs[r0 + width:r0 + 2 * width, 0:cols] = -imag_p
        rhs[r0 + width:r0 + 2 * width, cols:2 * cols] = real_p
    left = pt[...]
    for m in range(moms):
        real_f = ft_ref[m]
        imag_f = ft_ref[moms + m]
        pair = (jnp.concatenate([real_f, imag_f], axis=0), jnp.concatenate([imag_f, -real_f], axis=0))
        for c in range(2):
            value = dot(left, pair[c]).astype(BF16)
            for s in range(spins):
                at = (s * 2 + c) * width
                inner[:, at:at + width] = value[s * cols:(s + 1) * cols]
        both = dot(inner[...], rhs[...]).astype(BF16)
        out_ref[m, 0] = both[:, :cols]
        out_ref[m, 1] = both[:, cols:]


def sandwich_of(ft, peram, spins, cols):
    chunks, width, _ = ft.shape
    moms = chunks // 2
    vmem = pl.BlockSpec(memory_space=pltpu.VMEM)
    return pl.pallas_call(
        functools.partial(sandwich_kernel, moms, spins, cols),
        out_shape=jax.ShapeDtypeStruct((moms, 2, cols, cols), BF16),
        in_specs=[vmem, vmem],
        out_specs=vmem,
        scratch_shapes=[
            pltpu.VMEM((spins * cols, 2 * width), BF16),
            pltpu.VMEM((spins * 2 * width, 2 * cols), BF16),
            pltpu.VMEM((cols, spins * 2 * width), BF16),
        ],
        compiler_params=pltpu.CompilerParams(vmem_limit_bytes=32 << 20),
        name="sandwich",
    )(ft, peram)


def per_device(counts, vectors, gauge_links, momenta, perambulator):
    dims = vectors.shape[2:5]
    width = vectors.shape[5]
    moms = momenta.shape[0]
    plan = Plan(dims)
    sites = plan.sites
    cells = [dims[a] * counts[a] for a in range(3)]
    fields = vectors.reshape(6, sites, width)
    links = jnp.transpose(gauge_links.reshape(54, sites))
    links = jnp.pad(links, ((0, 0), (0, 128 - 54)))
    high = lax.reduce_precision(links, 8, 7)
    links = jnp.concatenate([high.astype(BF16), (links - high).astype(BF16)], axis=1)
    index = lax.broadcasted_iota(jnp.int32, (sites, 128), 0)
    lane = lax.broadcasted_iota(jnp.int32, (sites, 128), 1)
    spot = (index // (dims[1] * dims[2]), index // dims[2] % dims[1], index % dims[2])
    theta = jnp.zeros((sites, 128), F32)
    for a in range(3):
        at = lax.axis_index(AXES[a]) * dims[a] + spot[a]
        factor = jnp.zeros((sites, 128), jnp.int32)
        for m in range(moms):
            factor = jnp.where(lane // 2 == m, momenta[m, a], factor)
        theta = theta + (factor * at % cells[a]).astype(F32) / cells[a]
    theta = 2.0 * math.pi * theta
    tables = jnp.where(lane % 2 == 0, jnp.cos(theta), jnp.sin(theta))
    scale = 1.0 / math.sqrt(3.0 * cells[0] * cells[1] * cells[2])
    (smeared, ft), reduced = smear_and_project(plan, counts, scale, fields, links, tables, moms)
    if not reduced:
        ft = lax.psum(ft, AXES).astype(BF16)
    count, _, _, spins, cols = perambulator.shape
    rows = perambulator.reshape(count, 2, width, spins * cols)
    sandwich = jnp.stack([sandwich_of(ft, rows[n], spins, cols) for n in range(count)])
    return smeared.reshape(vectors.shape), sandwich


def solution(mesh):
    counts = tuple(mesh.shape[a] for a in AXES)
    return jax.shard_map(
        functools.partial(per_device, counts),
        mesh=mesh,
        in_specs=(
            P(None, None, "gx", "gy", "gz", None),
            P(None, None, None, None, "gx", "gy", "gz"),
            P(),
            P(("gx", "gy", "gz"), None, None, None, None),
        ),
        out_specs=(
            P(None, None, "gx", "gy", "gz", None),
            P(("gx", "gy", "gz"), None, None, None, None),
        ),
        check_vma=False,
    )
```

```python
import functools
import math

import jax
import jax.numpy as jnp
import numpy as np
from jax import lax
from jax.experimental import pallas as pl
from jax.experimental.pallas import tpu as pltpu
from jax.sharding import PartitionSpec as P

AXES = ("gx", "gy", "gz")
MESH = pl.DeviceIdType.MESH
F32 = jnp.float32
BF16 = jnp.bfloat16


class Plan:
    def __init__(self, dims):
        self.dims = dims
        self.sites = int(np.prod(dims))
        grid = np.indices(dims).reshape(3, -1)
        strides = (dims[1] * dims[2], dims[2], 1)
        self.face = [self.sites // dims[mu] for mu in range(3)]
        offset, self.slot = 0, []
        for mu in range(3):
            for _ in range(2):
                self.slot.append(offset)
                offset += self.face[mu]
        self.halo = offset
        self.cols = -(-(self.sites + offset) // 128) * 128
        offset, self.ghost = 0, []
        for mu in range(3):
            self.ghost.append(offset)
            offset += self.face[mu]
        self.ghosts = offset
        self.link_rows = -(-(self.sites + offset) // 16) * 16
        code = np.zeros((self.sites, self.cols), np.int32)
        pick = np.zeros((self.halo, self.sites), np.float32)
        pick_link = np.zeros((self.ghosts, self.sites), np.float32)
        below = np.zeros((3 * self.sites, self.link_rows), np.float32)
        for mu in range(3):
            others = [a for a in range(3) if a != mu]
            for s in range(self.sites):
                at = grid[:, s]
                f = at[others[0]] * dims[others[1]] + at[others[1]]
                if at[mu] == dims[mu] - 1:
                    code[s, self.sites + self.slot[2 * mu] + f] = 2 * mu + 1
                    pick[self.slot[2 * mu + 1] + f, s] = 1
                    pick_link[self.ghost[mu] + f, s] = 1
                else:
                    code[s, s + strides[mu]] = 2 * mu + 1
                if at[mu] == 0:
                    code[s, self.sites + self.slot[2 * mu + 1] + f] = 2 * mu + 2
                    pick[self.slot[2 * mu] + f, s] = 1
                    below[mu * self.sites + s, self.sites + self.ghost[mu] + f] = 1
                else:
                    code[s, s - strides[mu]] = 2 * mu + 2
                    below[mu * self.sites + s, s - strides[mu]] = 1
        self.code, self.pick, self.pick_link, self.below = code, pick, pick_link, below


def dot(a, b):
    return jnp.dot(a, b, preferred_element_type=F32)


def phase_table(plan, counts, me, mom_ref, moms):
    dims = plan.dims
    shape = (plan.sites, 128)
    site = lax.broadcasted_iota(jnp.int32, shape, 0).astype(F32)
    lane = lax.broadcasted_iota(jnp.int32, shape, 1)
    yz, zz = dims[1] * dims[2], dims[2]
    x = jnp.floor((site + 0.5) / yz)
    rest = site - x * yz
    y = jnp.floor((rest + 0.5) / zz)
    spot = (x, y, rest - y * zz)
    total = jnp.zeros(shape, F32)
    for a in range(3):
        at = spot[a] + (me[a] * dims[a]).astype(F32)
        cells = float(dims[a] * counts[a])
        factor = jnp.zeros(shape, F32)
        for m in range(moms):
            factor = jnp.where(lane >= 2 * m, mom_ref[m, a].astype(F32), factor)
        product = factor * at
        total = total + (product - jnp.floor(product / cells) * cells) / cells
    theta = 2.0 * math.pi * total
    return jnp.where(lane % 2 == 0, jnp.cos(theta), jnp.sin(theta))


def prepare(p_ref, pt_ref, rhs_ref, width):
    cols = rhs_ref.shape[1] // 2
    spins = pt_ref.shape[0] // cols
    for s in range(spins):
        real_p = p_ref[0, :, s * cols:(s + 1) * cols]
        imag_p = p_ref[1, :, s * cols:(s + 1) * cols]
        pt_ref[s * cols:(s + 1) * cols, 0:width] = jnp.transpose(real_p)
        pt_ref[s * cols:(s + 1) * cols, width:2 * width] = jnp.transpose(imag_p)
        r0 = s * 2 * width
        rhs_ref[r0:r0 + width, 0:cols] = real_p
        rhs_ref[r0:r0 + width, cols:2 * cols] = imag_p
        rhs_ref[r0 + width:r0 + 2 * width, 0:cols] = -imag_p
        rhs_ref[r0 + width:r0 + 2 * width, cols:2 * cols] = real_p


def main_kernel(plan, counts, scale, reduce_here, *refs):
    (v_ref, lt_ref, mom_ref, code_ref, pick_ref, pickl_ref, below_ref, p_ref,
     smeared_ref, out_ref, pt_ref, rhs_ref, tab, v1, v2, pk1, pk2, lk, lg, mh, ml, acc, half_out, half_in, plane_out, plane_in, z_out, z_in,
     ssem, rsem) = refs
    sites, cols, parts = plan.sites, plan.cols, 6
    me = [lax.axis_index(a) for a in AXES]
    nx, ny, nz = counts

    def neighbour(mu, step):
        at = list(me)
        at[mu] = lax.rem(at[mu] + step + counts[mu], counts[mu])
        return tuple(at)

    ny2 = ny // 2
    nq = nx * ny2
    h = lax.rem(me[1], 2)
    q = me[0] * ny2 + me[1] // 2
    partner = (me[0], me[1] + 1 - 2 * h, me[2])

    def plane_at(index):
        return (index // ny2, lax.rem(index, ny2) * 2 + h, me[2])

    greeted = [neighbour(mu, step) for mu in range(3) for step in (-1, 1)]
    if reduce_here:
        greeted += [partner]
        greeted += [plane_at(lax.rem(q + r, nq)) for r in range(1, nq)]
        greeted += [(me[0], me[1], lax.rem(me[2] + r, nz)) for r in range(1, nz)]
    barrier = pltpu.get_barrier_semaphore()
    for device in greeted:
        pl.semaphore_signal(barrier, inc=1, device_id=device, device_id_type=MESH)

    used = [0]

    def copy(src, dst, device):
        k = used[0]
        used[0] += 1
        return pltpu.make_async_remote_copy(
            src_ref=src, dst_ref=dst, send_sem=ssem.at[k], recv_sem=rsem.at[k],
            device_id=device, device_id_type=MESH)

    pick = pick_ref[...]

    def fill(buf, packed, part, value):
        buf[part, 0:sites, :] = value
        packed[part] = dot(pick, value).astype(BF16)

    rest = sites + plan.halo
    for buf in (v1, v2):
        if rest < cols:
            buf[:, rest:cols, :] = jnp.zeros((parts, cols - rest, buf.shape[2]), BF16)
    lt = lt_ref[...]
    lk[...] = dot(pickl_ref[...], lt).astype(BF16)
    lg[0:sites, :] = lt
    used_rows = sites + plan.ghosts
    if used_rows < plan.link_rows:
        lg[used_rows:, :] = jnp.zeros((plan.link_rows - used_rows, lg.shape[1]), BF16)
    for part in range(parts):
        fill(v1, pk1, part, v_ref[part])
    pl.semaphore_wait(barrier, len(greeted))

    sends = []
    links = []
    for mu in range(3):
        g, n = plan.ghost[mu], plan.face[mu]
        links.append(copy(lk.at[g:g + n, :], lg.at[sites + g:sites + g + n, :], neighbour(mu, 1)))
        links[-1].start()

    def exchange(packed, buf):
        made = []
        for mu in (2, 0, 1):
            for side in range(2):
                o, n = plan.slot[2 * mu + side], plan.face[mu]
                made.append(copy(packed.at[:, o:o + n, :],
                                 buf.at[:, sites + o:sites + o + n, :],
                                 neighbour(mu, 2 * side - 1)))
                made[-1].start()
        return made

    halo1 = exchange(pk1, v1)
    tab[...] = phase_table(plan, counts, me, mom_ref, out_ref.shape[0] // 2)
    for c in links:
        c.wait_recv()
    sends += links
    down = dot(below_ref[...], lg[...])
    here = lt.astype(F32)
    masks = [code_ref[...] == d + 1 for d in range(6)]
    shape = (sites, cols)
    for part, store in ((0, mh), (1, ml)):
        for i in range(3):
            for j in range(3):
                for c in range(2):
                    total = jnp.zeros(shape, F32)
                    for mu in range(3):
                        k = part * 128 + ((mu * 2 + c) * 3 + i) * 3 + j
                        value = here[:, k:k + 1]
                        total = jnp.where(masks[2 * mu], jnp.broadcast_to(value, shape), total)
                        k = part * 128 + ((mu * 2 + c) * 3 + j) * 3 + i
                        value = down[mu * sites:(mu + 1) * sites, k:k + 1]
                        if c:
                            value = -value
                        total = jnp.where(masks[2 * mu + 1], jnp.broadcast_to(value, shape), total)
                    total = total.astype(BF16)

                    def put(ro, co, val):
                        r0, c0 = (ro * 3 + i) * sites, (co * 3 + j) * cols
                        store[r0:r0 + sites, c0:c0 + cols] = val

                    if c == 0:
                        put(0, 0, total)
                        put(1, 1, total)
                    else:
                        put(1, 0, total)
                        put(0, 1, -total)

    def hop(buf):
        field = buf[...].reshape(parts * cols, buf.shape[2])
        return dot(mh[...], field) + dot(ml[...], field)

    for c in halo1:
        c.wait_recv()
    sends += halo1
    first = (hop(v1) / 6.0).astype(BF16)
    for part in range(parts):
        fill(v2, pk2, part, first[part * sites:(part + 1) * sites])
    halo2 = exchange(pk2, v2)
    for c in halo2:
        c.wait_recv()
    sends += halo2
    vectors = v_ref[...].reshape(parts * sites, v_ref.shape[2]).astype(F32)
    smeared = (2.0 * hop(v2) / 6.0 - vectors).astype(BF16)
    smeared_ref[...] = smeared.reshape(smeared_ref.shape)
    wide = smeared.astype(F32)
    rows = 3 * sites
    real_w, imag_w = wide[:rows], wide[rows:]
    left = jnp.transpose(wide).astype(BF16)
    moms = out_ref.shape[0] // 2
    width = v_ref.shape[2]
    for m in range(moms):
        cos_b = jnp.concatenate([tab[:, 2 * m:2 * m + 1]] * 3, axis=0)
        sin_b = jnp.concatenate([tab[:, 2 * m + 1:2 * m + 2]] * 3, axis=0)
        real_z = (cos_b * real_w + sin_b * imag_w).astype(BF16)
        imag_z = (cos_b * imag_w - sin_b * real_w).astype(BF16)
        acc[m] = dot(left, jnp.concatenate([real_z, imag_z], axis=0)) * scale
        acc[moms + m] = dot(left, jnp.concatenate([imag_z, -real_z], axis=0)) * scale

    if not reduce_here:
        prepare(p_ref, pt_ref, rhs_ref, width)
        out_ref[...] = acc[...]
        for c in sends:
            c.wait_send()
        return

    chunks = 2 * moms
    per = chunks // nz
    half = width // 2
    piece = half // nq
    keep = pl.multiple_of(h * half, half)
    give = pl.multiple_of((1 - h) * half, half)
    mine = pl.multiple_of(h * half + q * piece, piece)
    z = me[2]

    def plane_rows(p):
        return pl.ds(pl.multiple_of(h * half + p * piece, piece), piece)

    order = []
    for k in range(nz - 1):
        low = jnp.where(nz - 1 - k > z, nz - 1 - k, nz - 2 - k)
        high = jnp.where(k < z, k, k + 1)
        order.append(jnp.where(z < nz // 2, low, high))
    order.append(z)
    group = [pl.ds(p * per, per) for p in order]

    half_out[...] = acc[:, pl.ds(give, half), :].astype(BF16)
    pair = []
    for k in range(nz):
        pair.append(copy(half_out.at[group[k]], half_in.at[group[k]], partner))
        pair[-1].start()
    plane = []
    for k in range(nz):
        pair[k].wait_recv()
        total = acc[group[k], pl.ds(keep, half), :] + half_in[group[k]].astype(F32)
        acc[group[k], pl.ds(keep, half), :] = total
        plane_out[group[k]] = total.astype(BF16)
        row = []
        for r in range(1, nq):
            p = lax.rem(q + r, nq)
            row.append(copy(
                plane_out.at[group[k], pl.ds(pl.multiple_of(p * piece, piece), piece), :],
                plane_in.at[r - 1, group[k]], plane_at(p)))
            row[-1].start()
        plane.append(row)
    prepare(p_ref, pt_ref, rhs_ref, width)
    sends += pair
    base = used[0]
    for k in range(nz):
        total = acc[group[k], pl.ds(mine, piece), :]
        for r in range(1, nq):
            plane[k][r - 1].wait_recv()
            total = total + plane_in[r - 1, group[k]].astype(F32)
        sends += plane[k]
        if k < nz - 1:
            z_out[k] = total.astype(BF16)
            r = lax.rem(order[k] - z + nz, nz)
            c = pltpu.make_async_remote_copy(
                src_ref=z_out.at[k], dst_ref=z_in.at[r - 1], send_sem=ssem.at[base + k],
                recv_sem=rsem.at[base + r - 1], device_id=(me[0], me[1], order[k]),
                device_id_type=MESH)
            c.start()
            sends.append(c)
    used[0] += nz - 1
    for r in range(1, nz):
        pltpu.make_async_remote_copy(
            src_ref=z_out.at[r - 1], dst_ref=z_in.at[r - 1], send_sem=ssem.at[base + r - 1],
            recv_sem=rsem.at[base + r - 1], device_id=partner,
            device_id_type=MESH).wait_recv()
        total = total + z_in[r - 1].astype(F32)
    out_ref[group[nz - 1], pl.ds(mine, piece), :] = total.astype(BF16)

    def block(k, rows):
        return out_ref.at[group[k], rows, :]

    def arrival(ref, index):
        pltpu.make_async_remote_copy(
            src_ref=ref, dst_ref=ref, send_sem=ssem.at[index], recv_sem=rsem.at[index],
            device_id=partner, device_id_type=MESH).wait_recv()

    base = used[0]
    used[0] += nz - 1
    own = block(nz - 1, plane_rows(q))
    for k in range(nz - 1):
        r = lax.rem(order[k] - z + nz, nz)
        c = pltpu.make_async_remote_copy(
            src_ref=own, dst_ref=own, send_sem=ssem.at[base + k],
            recv_sem=rsem.at[base + r - 1], device_id=(me[0], me[1], order[k]),
            device_id_type=MESH)
        c.start()
        sends.append(c)
    spread = {}
    for k in reversed(range(nz)):
        if k < nz - 1:
            arrival(block(k, plane_rows(q)), base + lax.rem(z - order[k] + nz, nz) - 1)
        spread[k] = used[0]
        for r in range(1, nq):
            c = copy(block(k, plane_rows(q)), block(k, plane_rows(q)), plane_at(lax.rem(q + r, nq)))
            c.start()
            sends.append(c)
    pair = {}
    for k in reversed(range(nz)):
        for r in range(1, nq):
            arrival(block(k, plane_rows(lax.rem(q + nq - r, nq))), spread[k] + r - 1)
        pair[k] = used[0]
        c = copy(block(k, pl.ds(keep, half)), block(k, pl.ds(keep, half)), partner)
        c.start()
        sends.append(c)
    for k in reversed(range(nz)):
        arrival(block(k, pl.ds(give, half)), pair[k])
    for c in sends:
        c.wait_send()


def smear_and_project(plan, counts, scale, fields, links, momenta, rows, cols):
    moms = momenta.shape[0]
    parts, sites, width = fields.shape
    chunks = 2 * moms
    nx, ny, nz = counts
    nq = max(nx * (ny // 2), 1)
    half = width // 2
    reduce_here = ny % 2 == 0 and half % (16 * nq) == 0 and chunks % nz == 0 and nz > 1 and nq > 1
    vm = pltpu.VMEM
    if reduce_here:
        extra = [
            vm((chunks, half, width), BF16), vm((chunks, half, width), BF16),
            vm((chunks, half, width), BF16), vm((nq - 1, chunks, half // nq, width), BF16),
            vm((nz - 1, chunks // nz, half // nq, width), BF16),
            vm((nz - 1, chunks // nz, half // nq, width), BF16),
        ]
        copies = 3 + 12 + 2 * (nz + nz * (nq - 1) + (nz - 1))
    else:
        extra = [vm((8, 128), BF16)] * 6
        copies = 3 + 12
    vmem = pl.BlockSpec(memory_space=pltpu.VMEM)
    return pl.pallas_call(
        functools.partial(main_kernel, plan, counts, scale, reduce_here),
        out_shape=(
            jax.ShapeDtypeStruct((parts, sites, width), BF16),
            jax.ShapeDtypeStruct((chunks, width, width), BF16 if reduce_here else F32),
            jax.ShapeDtypeStruct((rows.shape[2], 2 * width), BF16),
            jax.ShapeDtypeStruct((rows.shape[2] // cols * 2 * width, 2 * cols), BF16),
        ),
        in_specs=[vmem, vmem, pl.BlockSpec(memory_space=pltpu.SMEM)] + [vmem] * 5,
        out_specs=(vmem,) * 4,
        scratch_shapes=[
            vm((sites, 128), F32),
            vm((parts, plan.cols, width), BF16), vm((parts, plan.cols, width), BF16),
            vm((parts, plan.halo, width), BF16), vm((parts, plan.halo, width), BF16),
            vm((plan.ghosts, 256), BF16), vm((plan.link_rows, 256), BF16),
            vm((parts * sites, parts * plan.cols), BF16),
            vm((parts * sites, parts * plan.cols), BF16),
            vm((chunks, width, width), F32),
            *extra,
            pltpu.SemaphoreType.DMA((copies,)), pltpu.SemaphoreType.DMA((copies,)),
        ],
        compiler_params=pltpu.CompilerParams(
            collective_id=0, has_side_effects=True, vmem_limit_bytes=48 << 20),
        name="smear_project",
    )(fields, links, momenta, jnp.asarray(plan.code), jnp.asarray(plan.pick, BF16),
      jnp.asarray(plan.pick_link, BF16), jnp.asarray(plan.below, BF16), rows), reduce_here


def sandwich_kernel(moms, spins, cols, ft_ref, pt, rhs, out_ref, inner):
    width = ft_ref.shape[1]
    left = pt[...]
    for m in range(moms):
        real_f = ft_ref[m]
        imag_f = ft_ref[moms + m]
        pair = (jnp.concatenate([real_f, imag_f], axis=0), jnp.concatenate([imag_f, -real_f], axis=0))
        for c in range(2):
            value = dot(left, pair[c]).astype(BF16)
            for s in range(spins):
                at = (s * 2 + c) * width
                inner[:, at:at + width] = value[s * cols:(s + 1) * cols]
        both = dot(inner[...], rhs[...]).astype(BF16)
        out_ref[m, 0] = both[:, :cols]
        out_ref[m, 1] = both[:, cols:]


def sandwich_of(ft, pt, rhs, spins, cols):
    chunks, width, _ = ft.shape
    moms = chunks // 2
    vmem = pl.BlockSpec(memory_space=pltpu.VMEM)
    return pl.pallas_call(
        functools.partial(sandwich_kernel, moms, spins, cols),
        out_shape=jax.ShapeDtypeStruct((moms, 2, cols, cols), BF16),
        in_specs=[vmem] * 3,
        out_specs=vmem,
        scratch_shapes=[
            pltpu.VMEM((cols, spins * 2 * width), BF16),
        ],
        compiler_params=pltpu.CompilerParams(vmem_limit_bytes=32 << 20),
        name="sandwich",
    )(ft, pt, rhs)


def prepare_one(rows, cols):
    width = rows.shape[1]
    spins = rows.shape[2] // cols
    vmem = pl.BlockSpec(memory_space=pltpu.VMEM)

    def kernel(p_ref, pt_ref, rhs_ref):
        prepare(p_ref, pt_ref, rhs_ref, width)

    return pl.pallas_call(
        kernel,
        out_shape=(
            jax.ShapeDtypeStruct((spins * cols, 2 * width), BF16),
            jax.ShapeDtypeStruct((spins * 2 * width, 2 * cols), BF16),
        ),
        in_specs=[vmem],
        out_specs=(vmem, vmem),
        name="prepare",
    )(rows)


def per_device(counts, vectors, gauge_links, momenta, perambulator):
    dims = vectors.shape[2:5]
    width = vectors.shape[5]
    plan = Plan(dims)
    sites = plan.sites
    cells = [dims[a] * counts[a] for a in range(3)]
    fields = vectors.reshape(6, sites, width)
    links = jnp.transpose(gauge_links.reshape(54, sites))
    links = jnp.pad(links, ((0, 0), (0, 128 - 54)))
    high = lax.reduce_precision(links, 8, 7)
    links = jnp.concatenate([high.astype(BF16), (links - high).astype(BF16)], axis=1)
    scale = 1.0 / math.sqrt(3.0 * cells[0] * cells[1] * cells[2])
    count, _, _, spins, cols = perambulator.shape
    rows = perambulator.reshape(count, 2, width, spins * cols)
    (smeared, ft, pt, rhs), reduced = smear_and_project(
        plan, counts, scale, fields, links, momenta, rows[0], cols)
    if not reduced:
        ft = lax.psum(ft, AXES).astype(BF16)
    sandwich = [sandwich_of(ft, pt, rhs, spins, cols)]
    for n in range(1, count):
        pt, rhs = prepare_one(rows[n], cols)
        sandwich.append(sandwich_of(ft, pt, rhs, spins, cols))
    sandwich = jnp.stack(sandwich)
    return smeared.reshape(vectors.shape), sandwich


def solution(mesh):
    counts = tuple(mesh.shape[a] for a in AXES)
    return jax.shard_map(
        functools.partial(per_device, counts),
        mesh=mesh,
        in_specs=(
            P(None, None, "gx", "gy", "gz", None),
            P(None, None, None, None, "gx", "gy", "gz"),
            P(),
            P(("gx", "gy", "gz"), None, None, None, None),
        ),
        out_specs=(
            P(None, None, "gx", "gy", "gz", None),
            P(("gx", "gy", "gz"), None, None, None, None),
        ),
        check_vma=False,
    )
```

```python
import functools
import math

import jax
import jax.numpy as jnp
import numpy as np
from jax import lax
from jax.experimental import pallas as pl
from jax.experimental.pallas import tpu as pltpu
from jax.sharding import PartitionSpec as P

AXES = ("gx", "gy", "gz")
MESH = pl.DeviceIdType.MESH
F32 = jnp.float32
BF16 = jnp.bfloat16


class Plan:
    def __init__(self, dims):
        self.dims = dims
        self.sites = int(np.prod(dims))
        grid = np.indices(dims).reshape(3, -1)
        strides = (dims[1] * dims[2], dims[2], 1)
        self.face = [self.sites // dims[mu] for mu in range(3)]
        offset, self.slot = 0, []
        for mu in range(3):
            for _ in range(2):
                self.slot.append(offset)
                offset += self.face[mu]
        self.halo = offset
        self.cols = -(-(self.sites + offset) // 128) * 128
        offset, self.ghost = 0, []
        for mu in range(3):
            self.ghost.append(offset)
            offset += self.face[mu]
        self.ghosts = offset
        self.link_rows = -(-(self.sites + offset) // 16) * 16
        code = np.zeros((self.sites, self.cols), np.int32)
        pick = np.zeros((self.halo, self.sites), np.float32)
        pick_link = np.zeros((self.ghosts, self.sites), np.float32)
        below = np.zeros((3 * self.sites, self.link_rows), np.float32)
        for mu in range(3):
            others = [a for a in range(3) if a != mu]
            for s in range(self.sites):
                at = grid[:, s]
                f = at[others[0]] * dims[others[1]] + at[others[1]]
                if at[mu] == dims[mu] - 1:
                    code[s, self.sites + self.slot[2 * mu] + f] = 2 * mu + 1
                    pick[self.slot[2 * mu + 1] + f, s] = 1
                    pick_link[self.ghost[mu] + f, s] = 1
                else:
                    code[s, s + strides[mu]] = 2 * mu + 1
                if at[mu] == 0:
                    code[s, self.sites + self.slot[2 * mu + 1] + f] = 2 * mu + 2
                    pick[self.slot[2 * mu] + f, s] = 1
                    below[mu * self.sites + s, self.sites + self.ghost[mu] + f] = 1
                else:
                    code[s, s - strides[mu]] = 2 * mu + 2
                    below[mu * self.sites + s, s - strides[mu]] = 1
        self.code, self.pick, self.pick_link, self.below = code, pick, pick_link, below


def dot(a, b):
    return jnp.dot(a, b, preferred_element_type=F32)


def phase_table(plan, counts, me, mom_ref, moms):
    dims = plan.dims
    shape = (plan.sites, 128)
    site = lax.broadcasted_iota(jnp.int32, shape, 0).astype(F32)
    lane = lax.broadcasted_iota(jnp.int32, shape, 1)
    yz, zz = dims[1] * dims[2], dims[2]
    x = jnp.floor((site + 0.5) / yz)
    rest = site - x * yz
    y = jnp.floor((rest + 0.5) / zz)
    spot = (x, y, rest - y * zz)
    total = jnp.zeros(shape, F32)
    for a in range(3):
        at = spot[a] + (me[a] * dims[a]).astype(F32)
        cells = float(dims[a] * counts[a])
        factor = jnp.zeros(shape, F32)
        for m in range(moms):
            factor = jnp.where(lane >= 2 * m, mom_ref[m, a].astype(F32), factor)
        product = factor * at
        total = total + (product - jnp.floor(product / cells) * cells) / cells
    theta = 2.0 * math.pi * total
    return jnp.where(lane % 2 == 0, jnp.cos(theta), jnp.sin(theta))


def prepare(p_ref, pt_ref, rhs_ref, width):
    cols = rhs_ref.shape[1] // 2
    spins = pt_ref.shape[0] // cols
    for s in range(spins):
        real_p = p_ref[0, :, s, :]
        imag_p = p_ref[1, :, s, :]
        pt_ref[s * cols:(s + 1) * cols, 0:width] = jnp.transpose(real_p)
        pt_ref[s * cols:(s + 1) * cols, width:2 * width] = jnp.transpose(imag_p)
        r0 = s * 2 * width
        rhs_ref[r0:r0 + width, 0:cols] = real_p
        rhs_ref[r0:r0 + width, cols:2 * cols] = imag_p
        rhs_ref[r0 + width:r0 + 2 * width, 0:cols] = -imag_p
        rhs_ref[r0 + width:r0 + 2 * width, cols:2 * cols] = real_p


def main_kernel(plan, counts, scale, reduce_here, *refs):
    (mom_ref, *hbm) = refs[:8]
    smeared_ref, result_ref, *local = refs[8:18]
    v_ref, lt_ref, code_ref, pick_ref, pickl_ref, below_ref, p_ref, isem = local
    (out_ref, pt_ref, rhs_ref, inner_ref, stage, tab, v1, v2, pk1, pk2, lk, lg, mh, ml, acc, half_out, half_in, plane_out, plane_in, z_out, z_in,
     ssem, rsem) = refs[18:]
    fetch = [pltpu.make_async_copy(hbm[k], local[k], isem.at[k]) for k in range(7)]
    for c in fetch:
        c.start()
    sites, cols, parts = plan.sites, plan.cols, 6
    me = [lax.axis_index(a) for a in AXES]
    nx, ny, nz = counts

    def neighbour(mu, step):
        at = list(me)
        at[mu] = lax.rem(at[mu] + step + counts[mu], counts[mu])
        return tuple(at)

    ny2 = ny // 2
    nq = nx * ny2
    h = lax.rem(me[1], 2)
    q = me[0] * ny2 + me[1] // 2
    partner = (me[0], me[1] + 1 - 2 * h, me[2])

    def plane_at(index):
        return (index // ny2, lax.rem(index, ny2) * 2 + h, me[2])

    greeted = [neighbour(mu, step) for mu in range(3) for step in (-1, 1)]
    if reduce_here:
        greeted += [partner]
        greeted += [plane_at(lax.rem(q + r, nq)) for r in range(1, nq)]
        greeted += [(me[0], me[1], lax.rem(me[2] + r, nz)) for r in range(1, nz)]
    barrier = pltpu.get_barrier_semaphore()
    for device in greeted:
        pl.semaphore_signal(barrier, inc=1, device_id=device, device_id_type=MESH)

    used = [0]

    def copy(src, dst, device):
        k = used[0]
        used[0] += 1
        return pltpu.make_async_remote_copy(
            src_ref=src, dst_ref=dst, send_sem=ssem.at[k], recv_sem=rsem.at[k],
            device_id=device, device_id_type=MESH)

    for c in fetch[:6]:
        c.wait()
    pick = pick_ref[...]

    def field_of(part):
        return v_ref[part // 3, part % 3].reshape(sites, v_ref.shape[-1])

    def fill(buf, packed, part, value):
        buf[part, 0:sites, :] = value
        packed[part] = dot(pick, value).astype(BF16)

    rest = sites + plan.halo
    for buf in (v1, v2):
        if rest < cols:
            buf[:, rest:cols, :] = jnp.zeros((parts, cols - rest, buf.shape[2]), BF16)
    stage[...] = jnp.zeros(stage.shape, F32)
    for x in range(plan.dims[0]):
        for y in range(plan.dims[1]):
            s0 = (x * plan.dims[1] + y) * plan.dims[2]
            stage[0:lt_ref.shape[0], s0:s0 + plan.dims[2]] = lt_ref[:, x, y, :]
    turned = jnp.transpose(stage[...])[0:sites]
    high = turned.astype(BF16)
    lt = jnp.concatenate([high, (turned - high.astype(F32)).astype(BF16)], axis=1)
    lk[...] = dot(pickl_ref[...], lt).astype(BF16)
    lg[0:sites, :] = lt
    used_rows = sites + plan.ghosts
    if used_rows < plan.link_rows:
        lg[used_rows:, :] = jnp.zeros((plan.link_rows - used_rows, lg.shape[1]), BF16)
    for part in range(parts):
        fill(v1, pk1, part, field_of(part))
    pl.semaphore_wait(barrier, len(greeted))

    sends = []
    links = []
    for mu in range(3):
        g, n = plan.ghost[mu], plan.face[mu]
        links.append(copy(lk.at[g:g + n, :], lg.at[sites + g:sites + g + n, :], neighbour(mu, 1)))
        links[-1].start()

    def exchange(packed, buf):
        made = []
        for mu in (2, 0, 1):
            for side in range(2):
                o, n = plan.slot[2 * mu + side], plan.face[mu]
                made.append(copy(packed.at[:, o:o + n, :],
                                 buf.at[:, sites + o:sites + o + n, :],
                                 neighbour(mu, 2 * side - 1)))
                made[-1].start()
        return made

    halo1 = exchange(pk1, v1)
    tab[...] = phase_table(plan, counts, me, mom_ref, mom_ref.shape[0])
    for c in links:
        c.wait_recv()
    sends += links
    down = dot(below_ref[...], lg[...])
    here = lt.astype(F32)
    masks = [code_ref[...] == d + 1 for d in range(6)]
    shape = (sites, cols)
    for part, store in ((0, mh), (1, ml)):
        for i in range(3):
            for j in range(3):
                for c in range(2):
                    total = jnp.zeros(shape, F32)
                    for mu in range(3):
                        k = part * 128 + ((mu * 2 + c) * 3 + i) * 3 + j
                        value = here[:, k:k + 1]
                        total = jnp.where(masks[2 * mu], jnp.broadcast_to(value, shape), total)
                        k = part * 128 + ((mu * 2 + c) * 3 + j) * 3 + i
                        value = down[mu * sites:(mu + 1) * sites, k:k + 1]
                        if c:
                            value = -value
                        total = jnp.where(masks[2 * mu + 1], jnp.broadcast_to(value, shape), total)
                    total = total.astype(BF16)

                    def put(ro, co, val):
                        r0, c0 = (ro * 3 + i) * sites, (co * 3 + j) * cols
                        store[r0:r0 + sites, c0:c0 + cols] = val

                    if c == 0:
                        put(0, 0, total)
                        put(1, 1, total)
                    else:
                        put(1, 0, total)
                        put(0, 1, -total)

    def hop(buf):
        field = buf[...].reshape(parts * cols, buf.shape[2])
        return dot(mh[...], field) + dot(ml[...], field)

    for c in halo1:
        c.wait_recv()
    sends += halo1
    first = (hop(v1) / 6.0).astype(BF16)
    for part in range(parts):
        fill(v2, pk2, part, first[part * sites:(part + 1) * sites])
    halo2 = exchange(pk2, v2)
    for c in halo2:
        c.wait_recv()
    sends += halo2
    vectors = v1[:, 0:sites, :].reshape(parts * sites, v1.shape[2]).astype(F32)
    smeared = (2.0 * hop(v2) / 6.0 - vectors).astype(BF16)
    smeared_ref[...] = smeared.reshape(smeared_ref.shape)
    wide = smeared.astype(F32)
    rows = 3 * sites
    real_w, imag_w = wide[:rows], wide[rows:]
    left = jnp.transpose(wide).astype(BF16)
    moms = mom_ref.shape[0]
    width = v1.shape[2]
    for m in range(moms):
        cos_b = jnp.concatenate([tab[:, 2 * m:2 * m + 1]] * 3, axis=0)
        sin_b = jnp.concatenate([tab[:, 2 * m + 1:2 * m + 2]] * 3, axis=0)
        real_z = (cos_b * real_w + sin_b * imag_w).astype(BF16)
        imag_z = (cos_b * imag_w - sin_b * real_w).astype(BF16)
        acc[m] = dot(left, jnp.concatenate([real_z, imag_z], axis=0)) * scale
        acc[moms + m] = dot(left, jnp.concatenate([imag_z, -real_z], axis=0)) * scale

    if not reduce_here:
        fetch[6].wait()
        result_ref[...] = acc[...]
        for c in sends:
            c.wait_send()
        return

    chunks = 2 * moms
    per = chunks // nz
    half = width // 2
    piece = half // nq
    keep = pl.multiple_of(h * half, half)
    give = pl.multiple_of((1 - h) * half, half)
    mine = pl.multiple_of(h * half + q * piece, piece)
    z = me[2]

    def plane_rows(p):
        return pl.ds(pl.multiple_of(h * half + p * piece, piece), piece)

    order = []
    for k in range(nz - 1):
        low = jnp.where(nz - 1 - k > z, nz - 1 - k, nz - 2 - k)
        high = jnp.where(k < z, k, k + 1)
        order.append(jnp.where(z < nz // 2, low, high))
    order.append(z)
    group = [pl.ds(p * per, per) for p in order]

    half_out[...] = acc[:, pl.ds(give, half), :].astype(BF16)
    pair = []
    for k in range(nz):
        pair.append(copy(half_out.at[group[k]], half_in.at[group[k]], partner))
        pair[-1].start()
    plane = []
    for k in range(nz):
        pair[k].wait_recv()
        total = acc[group[k], pl.ds(keep, half), :] + half_in[group[k]].astype(F32)
        acc[group[k], pl.ds(keep, half), :] = total
        plane_out[group[k]] = total.astype(BF16)
        row = []
        for r in range(1, nq):
            p = lax.rem(q + r, nq)
            row.append(copy(
                plane_out.at[group[k], pl.ds(pl.multiple_of(p * piece, piece), piece), :],
                plane_in.at[r - 1, group[k]], plane_at(p)))
            row[-1].start()
        plane.append(row)
    fetch[6].wait()
    prepare(p_ref, pt_ref, rhs_ref, width)
    sends += pair
    base = used[0]
    for k in range(nz):
        total = acc[group[k], pl.ds(mine, piece), :]
        for r in range(1, nq):
            plane[k][r - 1].wait_recv()
            total = total + plane_in[r - 1, group[k]].astype(F32)
        sends += plane[k]
        if k < nz - 1:
            z_out[k] = total.astype(BF16)
            r = lax.rem(order[k] - z + nz, nz)
            c = pltpu.make_async_remote_copy(
                src_ref=z_out.at[k], dst_ref=z_in.at[r - 1], send_sem=ssem.at[base + k],
                recv_sem=rsem.at[base + r - 1], device_id=(me[0], me[1], order[k]),
                device_id_type=MESH)
            c.start()
            sends.append(c)
    used[0] += nz - 1
    for r in range(1, nz):
        pltpu.make_async_remote_copy(
            src_ref=z_out.at[r - 1], dst_ref=z_in.at[r - 1], send_sem=ssem.at[base + r - 1],
            recv_sem=rsem.at[base + r - 1], device_id=partner,
            device_id_type=MESH).wait_recv()
        total = total + z_in[r - 1].astype(F32)
    out_ref[group[nz - 1], pl.ds(mine, piece), :] = total.astype(BF16)

    def block(k, rows):
        return out_ref.at[group[k], rows, :]

    def arrival(ref, index):
        pltpu.make_async_remote_copy(
            src_ref=ref, dst_ref=ref, send_sem=ssem.at[index], recv_sem=rsem.at[index],
            device_id=partner, device_id_type=MESH).wait_recv()

    base = used[0]
    used[0] += nz - 1
    own = block(nz - 1, plane_rows(q))
    for k in range(nz - 1):
        r = lax.rem(order[k] - z + nz, nz)
        c = pltpu.make_async_remote_copy(
            src_ref=own, dst_ref=own, send_sem=ssem.at[base + k],
            recv_sem=rsem.at[base + r - 1], device_id=(me[0], me[1], order[k]),
            device_id_type=MESH)
        c.start()
        sends.append(c)
    spread = {}
    for k in reversed(range(nz)):
        if k < nz - 1:
            arrival(block(k, plane_rows(q)), base + lax.rem(z - order[k] + nz, nz) - 1)
        spread[k] = used[0]
        for r in range(1, nq):
            c = copy(block(k, plane_rows(q)), block(k, plane_rows(q)), plane_at(lax.rem(q + r, nq)))
            c.start()
            sends.append(c)
    pair = {}
    for k in reversed(range(nz)):
        for r in range(1, nq):
            arrival(block(k, plane_rows(lax.rem(q + nq - r, nq))), spread[k] + r - 1)
        pair[k] = used[0]
        c = copy(block(k, pl.ds(keep, half)), block(k, pl.ds(keep, half)), partner)
        c.start()
        sends.append(c)
    for k in reversed(range(nz)):
        arrival(block(k, pl.ds(give, half)), pair[k])
    spins, cols = p_ref.shape[2:]
    sandwich_kernel(moms, spins, cols, out_ref, pt_ref, rhs_ref, result_ref, inner_ref)
    for c in sends:
        c.wait_send()


def smear_and_project(plan, counts, scale, vectors, links, momenta, peram):
    moms = momenta.shape[0]
    sites, width = plan.sites, vectors.shape[-1]
    parts, chunks = 6, 2 * moms
    count, _, _, spins, cols = peram.shape
    nx, ny, nz = counts
    nq = max(nx * (ny // 2), 1)
    half = width // 2
    reduce_here = (count == 1 and ny % 2 == 0 and half % (16 * nq) == 0 and chunks % nz == 0
                   and nz > 1 and nq > 1)
    vm = pltpu.VMEM
    if reduce_here:
        extra = [
            vm((chunks, half, width), BF16), vm((chunks, half, width), BF16),
            vm((chunks, half, width), BF16), vm((nq - 1, chunks, half // nq, width), BF16),
            vm((nz - 1, chunks // nz, half // nq, width), BF16),
            vm((nz - 1, chunks // nz, half // nq, width), BF16),
        ]
        copies = 3 + 12 + 2 * (nz + nz * (nq - 1) + (nz - 1))
        result = jax.ShapeDtypeStruct((moms, 2, cols, cols), BF16)
    else:
        extra = [vm((8, 128), BF16)] * 6
        copies = 3 + 12
        result = jax.ShapeDtypeStruct((chunks, width, width), F32)
    vmem = pl.BlockSpec(memory_space=pltpu.VMEM)
    operands = [vectors, links, jnp.asarray(plan.code), jnp.asarray(plan.pick, BF16),
                jnp.asarray(plan.pick_link, BF16), jnp.asarray(plan.below, BF16), peram[0]]
    return pl.pallas_call(
        functools.partial(main_kernel, plan, counts, scale, reduce_here),
        out_shape=(jax.ShapeDtypeStruct(vectors.shape, BF16), result),
        in_specs=[pl.BlockSpec(memory_space=pltpu.SMEM)]
        + [pl.BlockSpec(memory_space=pl.ANY)] * 7,
        out_specs=(vmem, vmem),
        scratch_shapes=[
            *[vm(a.shape, a.dtype) for a in operands], pltpu.SemaphoreType.DMA((7,)),
            vm((chunks, width, width), BF16), vm((spins * cols, 2 * width), BF16),
            vm((spins * 2 * width, 2 * cols), BF16), vm((cols, spins * 2 * width), BF16),
            vm((128, -(-sites // 128) * 128), F32),
            vm((sites, 128), F32),
            vm((parts, plan.cols, width), BF16), vm((parts, plan.cols, width), BF16),
            vm((parts, plan.halo, width), BF16), vm((parts, plan.halo, width), BF16),
            vm((plan.ghosts, 256), BF16), vm((plan.link_rows, 256), BF16),
            vm((parts * sites, parts * plan.cols), BF16),
            vm((parts * sites, parts * plan.cols), BF16),
            vm((chunks, width, width), F32),
            *extra,
            pltpu.SemaphoreType.DMA((copies,)), pltpu.SemaphoreType.DMA((copies,)),
        ],
        compiler_params=pltpu.CompilerParams(
            collective_id=0, has_side_effects=True, vmem_limit_bytes=60 << 20),
        name="smear_project",
    )(momenta, *operands), reduce_here


def sandwich_kernel(moms, spins, cols, ft_ref, pt, rhs, out_ref, inner):
    width = ft_ref.shape[1]
    left = pt[...]
    for m in range(moms):
        real_f = ft_ref[m]
        imag_f = ft_ref[moms + m]
        pair = (jnp.concatenate([real_f, imag_f], axis=0), jnp.concatenate([imag_f, -real_f], axis=0))
        for c in range(2):
            value = dot(left, pair[c]).astype(BF16)
            for s in range(spins):
                at = (s * 2 + c) * width
                inner[:, at:at + width] = value[s * cols:(s + 1) * cols]
        both = dot(inner[...], rhs[...]).astype(BF16)
        out_ref[m, 0] = both[:, :cols]
        out_ref[m, 1] = both[:, cols:]


def sandwich_of(ft, pt, rhs, spins, cols):
    chunks, width, _ = ft.shape
    moms = chunks // 2
    vmem = pl.BlockSpec(memory_space=pltpu.VMEM)
    return pl.pallas_call(
        functools.partial(sandwich_kernel, moms, spins, cols),
        out_shape=jax.ShapeDtypeStruct((moms, 2, cols, cols), BF16),
        in_specs=[vmem] * 3,
        out_specs=vmem,
        scratch_shapes=[
            pltpu.VMEM((cols, spins * 2 * width), BF16),
        ],
        compiler_params=pltpu.CompilerParams(vmem_limit_bytes=32 << 20),
        name="sandwich",
    )(ft, pt, rhs)


def prepare_one(rows):
    _, width, spins, cols = rows.shape
    vmem = pl.BlockSpec(memory_space=pltpu.VMEM)

    def kernel(p_ref, pt_ref, rhs_ref):
        prepare(p_ref, pt_ref, rhs_ref, width)

    return pl.pallas_call(
        kernel,
        out_shape=(
            jax.ShapeDtypeStruct((spins * cols, 2 * width), BF16),
            jax.ShapeDtypeStruct((spins * 2 * width, 2 * cols), BF16),
        ),
        in_specs=[vmem],
        out_specs=(vmem, vmem),
        name="prepare",
    )(rows)


def settled(*arrays):
    n = len(arrays)

    def kernel(*refs):
        held, sems = refs[2 * n:3 * n], refs[3 * n]
        into = [pltpu.make_async_copy(refs[k], held[k], sems.at[k]) for k in range(n)]
        back = [pltpu.make_async_copy(held[k], refs[n + k], sems.at[n + k]) for k in range(n)]
        for c in into:
            c.start()
        for c, d in zip(into, back):
            c.wait()
            d.start()
        for d in back:
            d.wait()

    return pl.pallas_call(
        kernel,
        out_shape=tuple(jax.ShapeDtypeStruct(a.shape, a.dtype) for a in arrays),
        in_specs=[pl.BlockSpec(memory_space=pl.ANY)] * n,
        out_specs=tuple(pl.BlockSpec(memory_space=pl.ANY) for _ in arrays),
        scratch_shapes=[*[pltpu.VMEM(a.shape, a.dtype) for a in arrays],
                        pltpu.SemaphoreType.DMA((2 * n,))],
        compiler_params=pltpu.CompilerParams(vmem_limit_bytes=60 << 20),
        name="settle",
    )(*arrays)


def per_device(counts, vectors, gauge_links, momenta, perambulator):
    dims = vectors.shape[2:5]
    plan = Plan(dims)
    sites = plan.sites
    cells = [dims[a] * counts[a] for a in range(3)]
    links = gauge_links.reshape((54,) + gauge_links.shape[4:])
    scale = 1.0 / math.sqrt(3.0 * cells[0] * cells[1] * cells[2])
    (smeared, result), finished = smear_and_project(
        plan, counts, scale, vectors, links, momenta, perambulator)
    if finished:
        smeared, result = settled(smeared, result)
        return smeared, result[None]
    ft = lax.psum(result, AXES).astype(BF16)
    count, _, _, spins, cols = perambulator.shape
    sandwich = []
    for n in range(count):
        pt, rhs = prepare_one(perambulator[n])
        sandwich.append(sandwich_of(ft, pt, rhs, spins, cols))
    return smeared, jnp.stack(sandwich)


def solution(mesh):
    counts = tuple(mesh.shape[a] for a in AXES)
    return jax.shard_map(
        functools.partial(per_device, counts),
        mesh=mesh,
        in_specs=(
            P(None, None, "gx", "gy", "gz", None),
            P(None, None, None, None, "gx", "gy", "gz"),
            P(),
            P(("gx", "gy", "gz"), None, None, None, None),
        ),
        out_specs=(
            P(None, None, "gx", "gy", "gz", None),
            P(("gx", "gy", "gz"), None, None, None, None),
        ),
        check_vma=False,
    )
```
